32 devices in a mesh: grp: 2 (over y), tm: 8 (over z, x), sens: 2 (over core).
Axes of the slice: x: 2, y: 2, z: 4, core: 2. Of those that a mesh axis runs over, the one named last changes fastest.
Arguments:
- features: bfloat16 [256, 2048, 128], P(('grp', 'sens'), 'tm'), parts along dimension 0, may hold values from -6 to 6
- target: float32 [256, 2048], P(('grp', 'sens'), 'tm'), parts along dimension 0, may hold values from -60 to 60
- test_matrix: float32 [2048, 64], P('tm'), may hold values from -0.125 to 0.125
- leading_conv_taps: bfloat16 [3, 2, 128, 128], replicated, may hold values from -0.375 to 0.375
- trailing_conv_taps: bfloat16 [3, 2, 128, 128], replicated, may hold values from -0.375 to 0.375
- readout: bfloat16 [128], replicated, may hold values from -0.5 to 0.5
- dilations: int32 [3], replicated, may hold values from 1 to 128, as said below
Outputs:
- remainder: float32 [256, 2048], P(('grp', 'sens'), 'tm'), parts along dimension 0
The draws below stay inside these ranges and needn't reach their ends.
There are 2 independent parts, one for each index of `grp`. The reference program is written for one: setup_inputs(seed, part) draws one part's arguments, and reference() takes and returns one part's arrays. A program takes and returns all parts, laid end to end along the dimension named above; an argument that names none is the same for every part. Nothing has to cross between parts.
Inputs may be any that keep to these rules, and one draw needn't show every extreme that they name: `dilations`: every dilation is a power of two, and the last block has dilation exactly 128.
All inputs are finite; a program needn't handle non-finite values.
Results may differ from the reference program's by a relative error of at most 0.0056.
Values may be sent and summed in bfloat16 or wider, within the bound.
A program may use at most 64 MiB of HBM per device.

```python
import math
import jax
import jax.numpy as jnp
from jax import lax

C = 128
K = 64
LAYERS = 3
DMAX = 128
SENSORS = 128
STEPS = 2048


def draw_target(key, part):
    first_key, second_key = jax.random.split(jax.random.fold_in(key, 11), 2)
    position = jnp.arange(STEPS, dtype=jnp.float32) / max(STEPS - 1, 1)
    ramp = 1.0 + 2.0 * position
    scales = 0.4 * jnp.exp(jax.random.uniform(second_key, (SENSORS, 1), jnp.float32, 0.0, math.log(10.0)))
    base = jnp.clip(jax.random.normal(first_key, (SENSORS, STEPS), jnp.float32), -4.0, 4.0)
    return (base * scales * ramp[None, :]).astype(jnp.float32)


def draw_dilations(key, part):
    top_power = DMAX.bit_length() - 1
    powers = jax.random.randint(jax.random.fold_in(key, 23), (LAYERS,), 0, top_power + 1)
    powers = jnp.where(jnp.arange(LAYERS) == LAYERS - 1, top_power, powers)
    return jnp.left_shift(jnp.ones((LAYERS,), jnp.int32), powers.astype(jnp.int32)).astype(jnp.int32)


def steps_of(own_key, shape, pieces, low, largest):
    level = 1.0
    for axis_at, parts in pieces:
        draws = jax.random.uniform(jax.random.fold_in(jax.random.fold_in(own_key, 6), axis_at), (parts,), jnp.float32, low / len(pieces), largest / len(pieces))
        level = level * jnp.repeat(jnp.exp(draws), shape[axis_at] // parts).reshape((-1,) + (1,) * (len(shape) - 1 - axis_at))
    return level


def normal_values(own_key, dims, spread, limit, pieces=(), held_as=jnp.bfloat16):
    result = spread * jax.random.normal(own_key, dims, jnp.float32)
    if pieces:
        result = result * steps_of(own_key, dims, pieces, -0.22, 0.18)
    return jnp.clip(result, -limit, limit).astype(held_as)


def setup_inputs(seed: int = 0, part: int = 0) -> dict:
    streams_of = jax.random.split(jax.random.key(seed), 8)
    part_keys = jax.random.split(jax.random.fold_in(streams_of[7], part), 8)
    features = normal_values(part_keys[0], (SENSORS, STEPS, C), 1.0, 6.0, ((0, 2), (1, 8)))
    target = draw_target(jax.random.fold_in(jax.random.fold_in(streams_of[7], part), 71), part)
    test_matrix = normal_values(streams_of[2], (STEPS, K), STEPS ** -0.5, 0.125, ((0, 8),), jnp.float32)
    leading_conv_taps = normal_values(streams_of[3], (LAYERS, 2, C, C), (2 * C) ** -0.5, 0.375)
    trailing_conv_taps = normal_values(streams_of[4], (LAYERS, 2, C, C), (2 * C) ** -0.5, 0.375)
    readout = normal_values(streams_of[5], (C,), C ** -0.5, 0.5)
    dilations = draw_dilations(jax.random.fold_in(streams_of[7], 71), part)
    return {"features": features, "target": target, "test_matrix": test_matrix, "leading_conv_taps": leading_conv_taps, "trailing_conv_taps": trailing_conv_taps, "readout": readout, "dilations": dilations}


def causal_conv(value, weight, dist):
    padded = jnp.pad(value, ((0, 0), (DMAX, 0), (0, 0)))
    moved = lax.dynamic_slice_in_dim(padded, (DMAX - dist).astype(jnp.int32), value.shape[1], 1)
    rows = value.shape[0] * value.shape[1]
    total = jnp.dot(moved.reshape(rows, C).astype(jnp.float32), weight[0].astype(jnp.float32), preferred_element_type=jnp.float32)
    total = total + jnp.dot(value.reshape(rows, C).astype(jnp.float32), weight[1].astype(jnp.float32), preferred_element_type=jnp.float32)
    return total.reshape(value.shape[0], value.shape[1], C)

def block_forecaster(residual_block, leading_conv_taps, trailing_conv_taps, readout, dilations):
    hidden = residual_block
    for layer in range(LAYERS):
        dist = dilations[layer]
        inner = jax.nn.relu(causal_conv(hidden, leading_conv_taps[layer], dist)).astype(jnp.bfloat16)
        branch = jax.nn.relu(causal_conv(inner, trailing_conv_taps[layer], dist))
        hidden = (hidden.astype(jnp.float32) + branch).astype(jnp.bfloat16)
    return jnp.einsum('stc,c->st', hidden.astype(jnp.float32), readout.astype(jnp.float32), preferred_element_type=jnp.float32)

def orthonormal(sketch):
    gram = jnp.dot(sketch.T, sketch, precision=lax.Precision.HIGHEST)
    factor = jnp.linalg.cholesky(gram)
    return jax.scipy.linalg.solve_triangular(factor, sketch.T, lower=True).T

def reference(features, target, test_matrix, leading_conv_taps, trailing_conv_taps, readout, dilations):
    block_list = features.reshape(SENSORS // 16, 16, STEPS, C)
    prediction_values = lax.map(lambda block_entry: block_forecaster(block_entry, leading_conv_taps, trailing_conv_taps, readout, dilations), block_list)
    resid = target - prediction_values.reshape(SENSORS, STEPS)
    high = lax.Precision.HIGHEST
    sketch = jnp.dot(resid, test_matrix, precision=high)
    basis = orthonormal(sketch)
    projected = jnp.dot(resid.T, basis, precision=high)
    sketch_two = jnp.dot(resid, projected, precision=high)
    basis_two = orthonormal(sketch_two)
    coef = jnp.dot(basis_two.T, resid, precision=high)
    return resid - jnp.dot(basis_two, coef, precision=high)
```

```python
import functools

import jax
import jax.numpy as jnp
from jax import lax
from jax.experimental import pallas as pl
from jax.experimental.pallas import tpu as pltpu
from jax.sharding import PartitionSpec as P

DMAX = 128
MESH = pl.DeviceIdType.MESH
HIGH = lax.Precision.HIGHEST


def shifted(value, axis, by):
    peers = lax.axis_size(axis)
    pairs = [(i, i + by) for i in range(peers) if 0 <= i + by < peers]
    return lax.ppermute(value, axis, pairs)


def dilated(before, current, dist, weight):
    extended = jnp.concatenate([before, current], axis=1)
    moved = lax.dynamic_slice_in_dim(extended, before.shape[1] - dist, current.shape[1], 1)
    total = jnp.einsum("stc,cd->std", moved, weight[0], preferred_element_type=jnp.float32)
    return total + jnp.einsum("stc,cd->std", current, weight[1], preferred_element_type=jnp.float32)


def causal_tail(value):
    return shifted(value[:, -DMAX:, :], "tm", 1)


def time_total(value):
    return lax.psum(value, "tm")


def joint_total(cross, sketch):
    return lax.psum((cross, jnp.dot(sketch.T, sketch, precision=HIGH)), "sens")


def lower_solve(factor, value):
    return jax.scipy.linalg.solve_triangular(factor, value, lower=True)


def halo_form(
    features, target, test_matrix, leading_conv_taps, trailing_conv_taps, readout, dilations
):
    hidden = features
    for layer in range(leading_conv_taps.shape[0]):
        dist = dilations[layer]
        inner = jax.nn.relu(
            dilated(causal_tail(hidden), hidden, dist, leading_conv_taps[layer])
        ).astype(jnp.bfloat16)
        branch = jax.nn.relu(dilated(causal_tail(inner), inner, dist, trailing_conv_taps[layer]))
        hidden = (hidden.astype(jnp.float32) + branch).astype(jnp.bfloat16)
    prediction_values = jnp.einsum("stc,c->st", hidden, readout, preferred_element_type=jnp.float32)
    resid = target - prediction_values
    sketch = time_total(jnp.dot(resid, test_matrix, precision=HIGH))
    cross, gram = joint_total(jnp.dot(resid.T, sketch, precision=HIGH), sketch)
    factor = jnp.linalg.cholesky(gram)
    projected = lower_solve(factor, cross.T).T
    sketch_two = time_total(jnp.dot(resid, projected, precision=HIGH))
    cross_two, gram_two = joint_total(jnp.dot(sketch_two.T, resid, precision=HIGH), sketch_two)
    factor_two = jnp.linalg.cholesky(gram_two)
    coef = lower_solve(factor_two, cross_two)
    basis_two = lower_solve(factor_two, sketch_two.T).T
    return resid - jnp.dot(basis_two, coef, precision=HIGH)


def exchange_kernel(
    peers, sides, chunk, rank,
    dil_ref, x_ref, tgt_ref, test_ref, lead_ref, trail_ref, read_ref,
    resid_ref, total_ref,
    recv, taps, pred, pred_in, tgt_in, part, part_in, red,
    own_sem, send_sem, recv_sem, tgt_send, tgt_recv, p_own, p_send, p_recv,
    s_own, s_send, s_recv, g_own, g_send, g_recv,
):
    me = lax.axis_index("tm")
    side = lax.axis_index("sens")
    other_side = 1 - side
    per = x_ref.shape[0] // peers
    steps = x_ref.shape[1]
    channels = x_ref.shape[2]
    chunks = per // chunk
    layers = lead_ref.shape[0]

    barrier = pltpu.get_barrier_semaphore()
    for k in range(1, peers):
        for s in range(sides):
            pl.semaphore_signal(barrier, inc=1, device_id={"tm": lax.rem(me + k, peers), "sens": lax.rem(side + s, sides)}, device_id_type=MESH)
    pl.semaphore_signal(barrier, inc=1, device_id={"sens": other_side}, device_id_type=MESH)
    pl.semaphore_wait(barrier, peers * sides - 1)

    def feature_copy(c, k):
        to = lax.rem(me + k, peers)
        return pltpu.make_async_remote_copy(
            src_ref=x_ref.at[pl.ds(to * per + c * chunk, chunk)],
            dst_ref=recv.at[c, me],
            send_sem=send_sem.at[c, k],
            recv_sem=recv_sem.at[c, me],
            device_id={"tm": to},
            device_id_type=MESH,
        )

    def feature_arrival(c, src):
        return pltpu.make_async_remote_copy(
            src_ref=x_ref.at[pl.ds(0, chunk)],
            dst_ref=recv.at[c, src],
            send_sem=send_sem.at[c, 1],
            recv_sem=recv_sem.at[c, src],
            device_id={"tm": lax.rem(me + 1, peers)},
            device_id_type=MESH,
        )

    def own_copy(c):
        return pltpu.make_async_copy(
            x_ref.at[pl.ds(me * per + c * chunk, chunk)], recv.at[c, me], recv_sem.at[c, me]
        )

    order = [peers // 2]
    for k in range(1, peers // 2):
        order += [peers // 2 - k, peers // 2 + k]
    for c in range(chunks):
        for k in order:
            feature_copy(c, k).start()
        own_copy(c).start()
    tgt_copy = pltpu.make_async_remote_copy(
        src_ref=tgt_ref, dst_ref=tgt_in, send_sem=tgt_send, recv_sem=tgt_recv,
        device_id={"sens": other_side}, device_id_type=MESH,
    )
    tgt_copy.start()

    for i in range(2 * layers):
        for s in range(chunk):
            taps[i, s, 0:DMAX, :] = jnp.zeros((DMAX, channels), jnp.float32)

    def conv(value, weight, i, j, dist):
        both = jnp.dot(value, weight, preferred_element_type=jnp.float32)
        start = DMAX + j * steps
        outs = []
        for s in range(chunk):
            taps[i, s, pl.ds(pl.multiple_of(start, DMAX), steps), :] = both[s * steps:(s + 1) * steps, :channels]
        for s in range(chunk):
            outs.append(taps[i, s, pl.ds(start - dist, steps), :])
        return jnp.concatenate(outs, axis=0) + both[:, channels:]

    def step(index, carry):
        c = index // peers
        j = index % peers
        feature_arrival(c, j).wait_recv()
        hidden = recv[c, j].reshape(chunk * steps, channels)
        for layer in range(layers):
            dist = dil_ref[layer]
            inner = jnp.maximum(conv(hidden, lead_ref[layer], 2 * layer, j, dist), 0.0).astype(jnp.bfloat16)
            branch = jnp.maximum(conv(inner, trail_ref[layer], 2 * layer + 1, j, dist), 0.0)
            hidden = (hidden.astype(jnp.float32) + branch).astype(jnp.bfloat16)
        for s in range(chunk):
            row = lax.dot_general(
                read_ref[...], hidden[s * steps:(s + 1) * steps], (((1,), (1,)), ((), ())),
                preferred_element_type=jnp.float32,
            )
            pred[j, pl.ds(c * chunk + s, 1), :] = row[0:1, :]
        return carry

    lax.fori_loop(0, chunks * peers, step, 0)

    def pred_copy(k, s):
        to = lax.rem(me + k, peers)
        return pltpu.make_async_remote_copy(
            src_ref=pred.at[to],
            dst_ref=pred_in.at[side * peers + me],
            send_sem=p_send.at[s, k],
            recv_sem=p_recv.at[side * peers + me],
            device_id={"tm": to, "sens": lax.rem(side + s, sides)},
            device_id_type=MESH,
        )

    everyone = [(k, s) for k in range(peers) for s in range(sides) if (k, s) != (0, 0)]
    for k, s in everyone:
        pred_copy(k, s).start()
    own_pred = pltpu.make_async_copy(pred.at[me], pred_in.at[side * peers + me], p_recv.at[side * peers + me])
    own_pred.start()
    tgt_copy.wait()
    for n in range(peers * sides):
        pltpu.make_async_remote_copy(
            src_ref=pred.at[0], dst_ref=pred_in.at[n], send_sem=p_send.at[0, 1], recv_sem=p_recv.at[n],
            device_id={"sens": other_side}, device_id_type=MESH,
        ).wait_recv()
    half = peers * per
    first = side == 0
    own_target = tgt_ref[...]
    far_target = tgt_in[...]
    low = jnp.where(first, own_target, far_target)
    high = jnp.where(first, far_target, own_target)
    everything = pred_in[...].reshape(sides * half, steps)
    resid = jnp.concatenate([low, high], axis=0) - everything
    resid_ref[...] = resid
    gram = lax.dot_general(resid, resid, (((1,), (1,)), ((), ())), precision=HIGH, preferred_element_type=jnp.float32)
    sketch = jnp.dot(resid, test_ref[...], precision=HIGH, preferred_element_type=jnp.float32)
    rows = part.shape[1]
    part[:, :, 0:sides * half] = gram.reshape(peers, rows, sides * half)
    part[:, :, sides * half:] = sketch.reshape(peers, rows, test_ref.shape[1])

    def sum_copy(k):
        to = lax.rem(me + k, peers)
        return pltpu.make_async_remote_copy(
            src_ref=part.at[to], dst_ref=part_in.at[me], send_sem=s_send.at[k], recv_sem=s_recv.at[me],
            device_id={"tm": to}, device_id_type=MESH,
        )

    def share_copy(k):
        to = lax.rem(me + k, peers)
        return pltpu.make_async_remote_copy(
            src_ref=red, dst_ref=total_ref.at[me], send_sem=g_send.at[k], recv_sem=g_recv.at[me],
            device_id={"tm": to}, device_id_type=MESH,
        )

    for k in range(1, peers):
        sum_copy(k).start()
    own_part = pltpu.make_async_copy(part.at[me], part_in.at[me], s_recv.at[me])
    own_part.start()
    acc = None
    for n in range(peers):
        pltpu.make_async_remote_copy(
            src_ref=part.at[0], dst_ref=part_in.at[n], send_sem=s_send.at[1], recv_sem=s_recv.at[n],
            device_id={"tm": lax.rem(me + 1, peers)}, device_id_type=MESH,
        ).wait_recv()
        acc = part_in[n] if acc is None else acc + part_in[n]
    red[...] = acc
    for k in range(1, peers):
        share_copy(k).start()
    own_red = pltpu.make_async_copy(red, total_ref.at[me], g_recv.at[me])
    own_red.start()
    for n in range(peers):
        pltpu.make_async_remote_copy(
            src_ref=red, dst_ref=total_ref.at[n], send_sem=g_send.at[1], recv_sem=g_recv.at[n],
            device_id={"tm": lax.rem(me + 1, peers)}, device_id_type=MESH,
        ).wait_recv()
    for k in range(1, peers):
        for c in range(chunks):
            feature_copy(c, k).wait_send()
        sum_copy(k).wait_send()
        share_copy(k).wait_send()
    for k, s in everyone:
        pred_copy(k, s).wait_send()


def orthonormal(sketch):
    rank = sketch.shape[1]
    gram = lax.dot_general(sketch, sketch, (((0,), (0,)), ((), ())), precision=HIGH, preferred_element_type=jnp.float32)
    row_of = lax.broadcasted_iota(jnp.int32, (rank, rank), 0)
    col_of = lax.broadcasted_iota(jnp.int32, (rank, rank), 1)
    eye = jnp.where(row_of == col_of, 1.0, 0.0).astype(jnp.float32)
    both = jnp.concatenate([gram, eye], axis=1)
    blocks = [both[8 * b:8 * b + 8] for b in range(rank // 8)]
    sub = lax.broadcasted_iota(jnp.int32, (8, 1), 0)
    for k in range(rank):
        top = k // 8
        pivot_row = blocks[top][k % 8:k % 8 + 1, :]
        inverse = 1.0 / pivot_row[:, k:k + 1]
        scaled = pivot_row * inverse
        for b in range(top, rank // 8):
            col = blocks[b][:, k:k + 1]
            if b == top:
                col = jnp.where(sub > k % 8, col, 0.0)
            blocks[b] = blocks[b] - col * scaled
    both = jnp.concatenate(blocks, axis=0)
    pivots = jnp.sum(jnp.where(row_of == col_of, both[:, :rank], 0.0), axis=1, keepdims=True)
    inverse_factor = both[:, rank:] * (1.0 / jnp.sqrt(pivots))
    return lax.dot_general(sketch, inverse_factor, (((1,), (1,)), ((), ())), precision=HIGH, preferred_element_type=jnp.float32)


def finish_kernel(own, resid_ref, total_ref, out_ref, basis_ref):
    side = lax.axis_index("sens")
    total = total_ref[...].reshape(resid_ref.shape[0], total_ref.shape[2])
    size = resid_ref.shape[0]
    gram = total[:, :size]
    basis = orthonormal(total[:, size:])
    sketch = jnp.dot(gram, basis, precision=HIGH, preferred_element_type=jnp.float32)
    basis = orthonormal(sketch)
    basis_ref[...] = basis
    resid = resid_ref[...]
    coef = lax.dot_general(basis, resid, (((0,), (0,)), ((), ())), precision=HIGH, preferred_element_type=jnp.float32)
    mine = pl.ds(pl.multiple_of(side * own, own), own)
    out_ref[...] = resid_ref[mine, :] - jnp.dot(basis_ref[mine, :], coef, precision=HIGH, preferred_element_type=jnp.float32)


def sensor_form(
    features, target, test_matrix, leading_conv_taps, trailing_conv_taps, readout, dilations
):
    peers = lax.axis_size("tm")
    sides = lax.axis_size("sens")
    own, steps, channels = features.shape
    rank = test_matrix.shape[1]
    layers = leading_conv_taps.shape[0]
    per = own // peers
    chunk = 2 if per % 2 == 0 else 1
    chunks = per // chunk
    size = own * sides
    lead = jnp.concatenate([leading_conv_taps[:, 0], leading_conv_taps[:, 1]], axis=-1)
    trail = jnp.concatenate([trailing_conv_taps[:, 0], trailing_conv_taps[:, 1]], axis=-1)
    read = jnp.broadcast_to(readout[None, :], (16, channels))
    vmem = pl.BlockSpec(memory_space=pltpu.VMEM)
    dma = pltpu.SemaphoreType.DMA
    resid, total = pl.pallas_call(
        functools.partial(exchange_kernel, peers, sides, chunk, rank),
        out_shape=(
            jax.ShapeDtypeStruct((size, steps), jnp.float32),
            jax.ShapeDtypeStruct((peers, size // peers, size + rank), jnp.float32),
        ),
        in_specs=[
            pl.BlockSpec(memory_space=pltpu.SMEM), pl.BlockSpec(memory_space=pl.ANY),
            vmem, vmem, vmem, vmem, vmem,
        ],
        out_specs=(vmem, vmem),
        scratch_shapes=[
            pltpu.VMEM((chunks, peers, chunk, steps, channels), jnp.bfloat16),
            pltpu.VMEM((2 * layers, chunk, DMAX + peers * steps, channels), jnp.float32),
            pltpu.VMEM((peers, per, steps), jnp.float32),
            pltpu.VMEM((peers * sides, per, steps), jnp.float32),
            pltpu.VMEM((own, steps), jnp.float32),
            pltpu.VMEM((peers, size // peers, size + rank), jnp.float32),
            pltpu.VMEM((peers, size // peers, size + rank), jnp.float32),
            pltpu.VMEM((size // peers, size + rank), jnp.float32),
            dma, dma((chunks, peers)), dma((chunks, peers)), dma, dma,
            dma, dma((sides, peers)), dma((peers * sides,)),
            dma, dma((peers,)), dma((peers,)),
            dma, dma((peers,)), dma((peers,)),
        ],
        compiler_params=pltpu.CompilerParams(
            collective_id=0, has_side_effects=True, vmem_limit_bytes=56 * 1024 * 1024
        ),
        name="exchange",
    )(dilations, features, target, test_matrix, lead, trail, read)
    return pl.pallas_call(
        functools.partial(finish_kernel, own),
        out_shape=jax.ShapeDtypeStruct((own, steps), jnp.float32),
        in_specs=[vmem, vmem],
        out_specs=vmem,
        scratch_shapes=[pltpu.VMEM((size, rank), jnp.float32)],
        name="finish",
    )(resid, total)


def on_device(features, *rest):
    peers = lax.axis_size("tm")
    if lax.axis_size("sens") == 2 and features.shape[0] % (8 * peers) == 0:
        return sensor_form(features, *rest)
    return halo_form(features, *rest)


def solution(mesh):
    placed = (
        P(("grp", "sens"), "tm", None),
        P(("grp", "sens"), "tm"),
        P("tm", None),
        P(),
        P(),
        P(),
        P(),
    )
    return jax.shard_map(
        on_device, mesh=mesh, in_specs=placed, out_specs=P(("grp", "sens"), "tm"), check_vma=False
    )
```

```python
import functools

import jax
import jax.numpy as jnp
from jax import lax
from jax.experimental import pallas as pl
from jax.experimental.pallas import tpu as pltpu
from jax.sharding import PartitionSpec as P

DMAX = 128
MESH = pl.DeviceIdType.MESH
HIGH = lax.Precision.HIGHEST


def shifted(value, axis, by):
    peers = lax.axis_size(axis)
    pairs = [(i, i + by) for i in range(peers) if 0 <= i + by < peers]
    return lax.ppermute(value, axis, pairs)


def dilated(before, current, dist, weight):
    extended = jnp.concatenate([before, current], axis=1)
    moved = lax.dynamic_slice_in_dim(extended, before.shape[1] - dist, current.shape[1], 1)
    total = jnp.einsum("stc,cd->std", moved, weight[0], preferred_element_type=jnp.float32)
    return total + jnp.einsum("stc,cd->std", current, weight[1], preferred_element_type=jnp.float32)


def causal_tail(value):
    return shifted(value[:, -DMAX:, :], "tm", 1)


def time_total(value):
    return lax.psum(value, "tm")


def joint_total(cross, sketch):
    return lax.psum((cross, jnp.dot(sketch.T, sketch, precision=HIGH)), "sens")


def lower_solve(factor, value):
    return jax.scipy.linalg.solve_triangular(factor, value, lower=True)


def halo_form(
    features, target, test_matrix, leading_conv_taps, trailing_conv_taps, readout, dilations
):
    hidden = features
    for layer in range(leading_conv_taps.shape[0]):
        dist = dilations[layer]
        inner = jax.nn.relu(
            dilated(causal_tail(hidden), hidden, dist, leading_conv_taps[layer])
        ).astype(jnp.bfloat16)
        branch = jax.nn.relu(dilated(causal_tail(inner), inner, dist, trailing_conv_taps[layer]))
        hidden = (hidden.astype(jnp.float32) + branch).astype(jnp.bfloat16)
    prediction_values = jnp.einsum("stc,c->st", hidden, readout, preferred_element_type=jnp.float32)
    resid = target - prediction_values
    sketch = time_total(jnp.dot(resid, test_matrix, precision=HIGH))
    cross, gram = joint_total(jnp.dot(resid.T, sketch, precision=HIGH), sketch)
    factor = jnp.linalg.cholesky(gram)
    projected = lower_solve(factor, cross.T).T
    sketch_two = time_total(jnp.dot(resid, projected, precision=HIGH))
    cross_two, gram_two = joint_total(jnp.dot(sketch_two.T, resid, precision=HIGH), sketch_two)
    factor_two = jnp.linalg.cholesky(gram_two)
    coef = lower_solve(factor_two, cross_two)
    basis_two = lower_solve(factor_two, sketch_two.T).T
    return resid - jnp.dot(basis_two, coef, precision=HIGH)


def exchange_kernel(
    peers, sides, chunk, rank,
    dil_ref, x_ref, tgt_ref, test_ref, lead_ref, trail_ref, read_ref,
    resid_ref, total_ref,
    recv, taps, pred, pred_in, tgt_in, part, part_in, red,
    own_sem, send_sem, recv_sem, tgt_send, tgt_recv, p_own, p_send, p_recv,
    s_own, s_send, s_recv, g_own, g_send, g_recv,
):
    me = lax.axis_index("tm")
    side = lax.axis_index("sens")
    other_side = 1 - side
    per = x_ref.shape[0] // peers
    steps = x_ref.shape[1]
    channels = x_ref.shape[2]
    chunks = per // chunk
    layers = lead_ref.shape[0]

    barrier = pltpu.get_barrier_semaphore()
    for k in range(1, peers):
        for s in range(sides):
            pl.semaphore_signal(barrier, inc=1, device_id={"tm": lax.rem(me + k, peers), "sens": lax.rem(side + s, sides)}, device_id_type=MESH)
    pl.semaphore_signal(barrier, inc=1, device_id={"sens": other_side}, device_id_type=MESH)
    pl.semaphore_wait(barrier, peers * sides - 1)

    def feature_copy(c, k):
        to = lax.rem(me + k, peers)
        return pltpu.make_async_remote_copy(
            src_ref=x_ref.at[pl.ds(to * per + c * chunk, chunk)],
            dst_ref=recv.at[c, me],
            send_sem=send_sem.at[c, k],
            recv_sem=recv_sem.at[c, me],
            device_id={"tm": to},
            device_id_type=MESH,
        )

    def feature_arrival(c, src):
        return pltpu.make_async_remote_copy(
            src_ref=x_ref.at[pl.ds(0, chunk)],
            dst_ref=recv.at[c, src],
            send_sem=send_sem.at[c, 1],
            recv_sem=recv_sem.at[c, src],
            device_id={"tm": lax.rem(me + 1, peers)},
            device_id_type=MESH,
        )

    def own_copy(c):
        return pltpu.make_async_copy(
            x_ref.at[pl.ds(me * per + c * chunk, chunk)], recv.at[c, me], recv_sem.at[c, me]
        )

    order = [peers // 2]
    for k in range(1, peers // 2):
        order += [peers // 2 - k, peers // 2 + k]
    for c in range(chunks):
        for k in order:
            feature_copy(c, k).start()
        own_copy(c).start()
    tgt_copy = pltpu.make_async_remote_copy(
        src_ref=tgt_ref, dst_ref=tgt_in, send_sem=tgt_send, recv_sem=tgt_recv,
        device_id={"sens": other_side}, device_id_type=MESH,
    )
    tgt_copy.start()

    for i in range(2 * layers):
        for s in range(chunk):
            taps[i, s, 0:DMAX, :] = jnp.zeros((DMAX, channels), jnp.float32)

    read = jnp.broadcast_to(read_ref[...], (16, channels))

    def conv(value, weight, i, j, dist):
        start = DMAX + j * steps
        wide = value.astype(jnp.float32)
        outs = []
        for s in range(chunk):
            taps[i, s, pl.ds(pl.multiple_of(start, DMAX), steps), :] = wide[s * steps:(s + 1) * steps]
        for s in range(chunk):
            outs.append(taps[i, s, pl.ds(start - dist, steps), :].astype(jnp.bfloat16))
        joined = jnp.concatenate([jnp.concatenate(outs, axis=0), value], axis=1)
        return jnp.dot(joined, weight, preferred_element_type=jnp.float32)

    def step(index, carry):
        c = index // peers
        j = index % peers
        feature_arrival(c, j).wait_recv()
        hidden = recv[c, j].reshape(chunk * steps, channels)
        for layer in range(layers):
            dist = dil_ref[layer]
            inner = jnp.maximum(conv(hidden, lead_ref[layer], 2 * layer, j, dist), 0.0).astype(jnp.bfloat16)
            branch = jnp.maximum(conv(inner, trail_ref[layer], 2 * layer + 1, j, dist), 0.0)
            hidden = (hidden.astype(jnp.float32) + branch).astype(jnp.bfloat16)
        for s in range(chunk):
            row = lax.dot_general(
                read, hidden[s * steps:(s + 1) * steps], (((1,), (1,)), ((), ())),
                preferred_element_type=jnp.float32,
            )
            pred[j, pl.ds(c * chunk + s, 1), :] = row[0:1, :]
        return carry

    lax.fori_loop(0, chunks * peers, step, 0)

    def pred_copy(k, s):
        to = lax.rem(me + k, peers)
        return pltpu.make_async_remote_copy(
            src_ref=pred.at[to],
            dst_ref=pred_in.at[side * peers + me],
            send_sem=p_send.at[s, k],
            recv_sem=p_recv.at[side * peers + me],
            device_id={"tm": to, "sens": lax.rem(side + s, sides)},
            device_id_type=MESH,
        )

    everyone = [(k, s) for k in range(peers) for s in range(sides) if (k, s) != (0, 0)]
    for k, s in everyone:
        pred_copy(k, s).start()
    own_pred = pltpu.make_async_copy(pred.at[me], pred_in.at[side * peers + me], p_recv.at[side * peers + me])
    own_pred.start()
    tgt_copy.wait()
    for n in range(peers * sides):
        pltpu.make_async_remote_copy(
            src_ref=pred.at[0], dst_ref=pred_in.at[n], send_sem=p_send.at[0, 1], recv_sem=p_recv.at[n],
            device_id={"sens": other_side}, device_id_type=MESH,
        ).wait_recv()
    half = peers * per
    first = side == 0
    own_target = tgt_ref[...]
    far_target = tgt_in[...]
    low = jnp.where(first, own_target, far_target)
    high = jnp.where(first, far_target, own_target)
    everything = pred_in[...].reshape(sides * half, steps)
    resid = jnp.concatenate([low, high], axis=0) - everything
    resid_ref[...] = resid
    gram = lax.dot_general(resid, resid, (((1,), (1,)), ((), ())), precision=HIGH, preferred_element_type=jnp.float32)
    sketch = lax.dot_general(resid, test_ref[...], (((1,), (1,)), ((), ())), precision=HIGH, preferred_element_type=jnp.float32)
    rows = part.shape[1]
    part[:, :, 0:sides * half] = gram.reshape(peers, rows, sides * half)
    part[:, :, sides * half:] = sketch.reshape(peers, rows, rank)

    def sum_copy(k):
        to = lax.rem(me + k, peers)
        return pltpu.make_async_remote_copy(
            src_ref=part.at[to], dst_ref=part_in.at[me], send_sem=s_send.at[k], recv_sem=s_recv.at[me],
            device_id={"tm": to}, device_id_type=MESH,
        )

    def share_copy(k):
        to = lax.rem(me + k, peers)
        return pltpu.make_async_remote_copy(
            src_ref=red, dst_ref=total_ref.at[me], send_sem=g_send.at[k], recv_sem=g_recv.at[me],
            device_id={"tm": to}, device_id_type=MESH,
        )

    for k in range(1, peers):
        sum_copy(k).start()
    own_part = pltpu.make_async_copy(part.at[me], part_in.at[me], s_recv.at[me])
    own_part.start()
    acc = None
    for n in range(peers):
        pltpu.make_async_remote_copy(
            src_ref=part.at[0], dst_ref=part_in.at[n], send_sem=s_send.at[1], recv_sem=s_recv.at[n],
            device_id={"tm": lax.rem(me + 1, peers)}, device_id_type=MESH,
        ).wait_recv()
        acc = part_in[n] if acc is None else acc + part_in[n]
    red[...] = acc
    for k in range(1, peers):
        share_copy(k).start()
    own_red = pltpu.make_async_copy(red, total_ref.at[me], g_recv.at[me])
    own_red.start()
    for n in range(peers):
        pltpu.make_async_remote_copy(
            src_ref=red, dst_ref=total_ref.at[n], send_sem=g_send.at[1], recv_sem=g_recv.at[n],
            device_id={"tm": lax.rem(me + 1, peers)}, device_id_type=MESH,
        ).wait_recv()
    for k in range(1, peers):
        for c in range(chunks):
            feature_copy(c, k).wait_send()
        sum_copy(k).wait_send()
        share_copy(k).wait_send()
    for k, s in everyone:
        pred_copy(k, s).wait_send()


def orthonormal(sketch):
    rank = sketch.shape[1]
    gram = lax.dot_general(sketch, sketch, (((0,), (0,)), ((), ())), precision=HIGH, preferred_element_type=jnp.float32)
    row_of = lax.broadcasted_iota(jnp.int32, (rank, rank), 0)
    col_of = lax.broadcasted_iota(jnp.int32, (rank, rank), 1)
    eye = jnp.where(row_of == col_of, 1.0, 0.0).astype(jnp.float32)
    both = jnp.concatenate([gram, eye], axis=1)
    blocks = [both[8 * b:8 * b + 8] for b in range(rank // 8)]
    sub = lax.broadcasted_iota(jnp.int32, (8, 1), 0)
    for k in range(rank):
        top = k // 8
        pivot_row = blocks[top][k % 8:k % 8 + 1, :]
        inverse = 1.0 / pivot_row[:, k:k + 1]
        scaled = pivot_row * inverse
        for b in range(top, rank // 8):
            col = blocks[b][:, k:k + 1]
            if b == top:
                col = jnp.where(sub > k % 8, col, 0.0)
            blocks[b] = blocks[b] - col * scaled
    both = jnp.concatenate(blocks, axis=0)
    pivots = jnp.sum(jnp.where(row_of == col_of, both[:, :rank], 0.0), axis=1, keepdims=True)
    inverse_factor = both[:, rank:] * (1.0 / jnp.sqrt(pivots))
    return lax.dot_general(sketch, inverse_factor, (((1,), (1,)), ((), ())), precision=HIGH, preferred_element_type=jnp.float32)


def finish_kernel(own, resid_ref, total_ref, out_ref, basis_ref):
    side = lax.axis_index("sens")
    total = total_ref[...].reshape(resid_ref.shape[0], total_ref.shape[2])
    size = resid_ref.shape[0]
    gram = total[:, :size]
    basis = orthonormal(total[:, size:])
    sketch = jnp.dot(gram, basis, precision=HIGH, preferred_element_type=jnp.float32)
    basis = orthonormal(sketch)
    basis_ref[...] = basis
    resid = resid_ref[...]
    coef = lax.dot_general(basis, resid, (((0,), (0,)), ((), ())), precision=HIGH, preferred_element_type=jnp.float32)
    mine = pl.ds(pl.multiple_of(side * own, own), own)
    out_ref[...] = resid_ref[mine, :] - jnp.dot(basis_ref[mine, :], coef, precision=HIGH, preferred_element_type=jnp.float32)


def sensor_form(
    features, target, test_matrix, leading_conv_taps, trailing_conv_taps, readout, dilations
):
    peers = lax.axis_size("tm")
    sides = lax.axis_size("sens")
    own, steps, channels = features.shape
    rank = test_matrix.shape[1]
    layers = leading_conv_taps.shape[0]
    per = own // peers
    chunk = 2 if per % 2 == 0 else 1
    chunks = per // chunk
    size = own * sides
    lead = leading_conv_taps.reshape(layers, 2 * channels, channels)
    trail = trailing_conv_taps.reshape(layers, 2 * channels, channels)
    read = readout.reshape(1, channels)
    vmem = pl.BlockSpec(memory_space=pltpu.VMEM)
    dma = pltpu.SemaphoreType.DMA
    resid, total = pl.pallas_call(
        functools.partial(exchange_kernel, peers, sides, chunk, rank),
        out_shape=(
            jax.ShapeDtypeStruct((size, steps), jnp.float32),
            jax.ShapeDtypeStruct((peers, size // peers, size + rank), jnp.float32),
        ),
        in_specs=[
            pl.BlockSpec(memory_space=pltpu.SMEM), pl.BlockSpec(memory_space=pl.ANY),
            vmem, vmem, vmem, vmem, vmem,
        ],
        out_specs=(vmem, vmem),
        scratch_shapes=[
            pltpu.VMEM((chunks, peers, chunk, steps, channels), jnp.bfloat16),
            pltpu.VMEM((2 * layers, chunk, DMAX + peers * steps, channels), jnp.float32),
            pltpu.VMEM((peers, per, steps), jnp.float32),
            pltpu.VMEM((peers * sides, per, steps), jnp.float32),
            pltpu.VMEM((own, steps), jnp.float32),
            pltpu.VMEM((peers, size // peers, size + rank), jnp.float32),
            pltpu.VMEM((peers, size // peers, size + rank), jnp.float32),
            pltpu.VMEM((size // peers, size + rank), jnp.float32),
            dma, dma((chunks, peers)), dma((chunks, peers)), dma, dma,
            dma, dma((sides, peers)), dma((peers * sides,)),
            dma, dma((peers,)), dma((peers,)),
            dma, dma((peers,)), dma((peers,)),
        ],
        compiler_params=pltpu.CompilerParams(
            collective_id=0, has_side_effects=True, vmem_limit_bytes=56 * 1024 * 1024
        ),
        name="exchange",
    )(dilations, features, target, test_matrix.T, lead, trail, read)
    return pl.pallas_call(
        functools.partial(finish_kernel, own),
        out_shape=jax.ShapeDtypeStruct((own, steps), jnp.float32),
        in_specs=[vmem, vmem],
        out_specs=vmem,
        scratch_shapes=[pltpu.VMEM((size, rank), jnp.float32)],
        name="finish",
    )(resid, total)


def on_device(features, *rest):
    peers = lax.axis_size("tm")
    if lax.axis_size("sens") == 2 and features.shape[0] % (8 * peers) == 0:
        return sensor_form(features, *rest)
    return halo_form(features, *rest)


def solution(mesh):
    placed = (
        P(("grp", "sens"), "tm", None),
        P(("grp", "sens"), "tm"),
        P("tm", None),
        P(),
        P(),
        P(),
        P(),
    )
    return jax.shard_map(
        on_device, mesh=mesh, in_specs=placed, out_specs=P(("grp", "sens"), "tm"), check_vma=False
    )
```

```python
import functools

import jax
import jax.numpy as jnp
from jax import lax
from jax.experimental import pallas as pl
from jax.experimental.pallas import tpu as pltpu
from jax.sharding import PartitionSpec as P

DMAX = 128
MESH = pl.DeviceIdType.MESH
HIGH = lax.Precision.HIGHEST


def shifted(value, axis, by):
    peers = lax.axis_size(axis)
    pairs = [(i, i + by) for i in range(peers) if 0 <= i + by < peers]
    return lax.ppermute(value, axis, pairs)


def dilated(before, current, dist, weight):
    extended = jnp.concatenate([before, current], axis=1)
    moved = lax.dynamic_slice_in_dim(extended, before.shape[1] - dist, current.shape[1], 1)
    total = jnp.einsum("stc,cd->std", moved, weight[0], preferred_element_type=jnp.float32)
    return total + jnp.einsum("stc,cd->std", current, weight[1], preferred_element_type=jnp.float32)


def causal_tail(value):
    return shifted(value[:, -DMAX:, :], "tm", 1)


def time_total(value):
    return lax.psum(value, "tm")


def joint_total(cross, sketch):
    return lax.psum((cross, jnp.dot(sketch.T, sketch, precision=HIGH)), "sens")


def lower_solve(factor, value):
    return jax.scipy.linalg.solve_triangular(factor, value, lower=True)


def halo_form(
    features, target, test_matrix, leading_conv_taps, trailing_conv_taps, readout, dilations
):
    hidden = features
    for layer in range(leading_conv_taps.shape[0]):
        dist = dilations[layer]
        inner = jax.nn.relu(
            dilated(causal_tail(hidden), hidden, dist, leading_conv_taps[layer])
        ).astype(jnp.bfloat16)
        branch = jax.nn.relu(dilated(causal_tail(inner), inner, dist, trailing_conv_taps[layer]))
        hidden = (hidden.astype(jnp.float32) + branch).astype(jnp.bfloat16)
    prediction_values = jnp.einsum("stc,c->st", hidden, readout, preferred_element_type=jnp.float32)
    resid = target - prediction_values
    sketch = time_total(jnp.dot(resid, test_matrix, precision=HIGH))
    cross, gram = joint_total(jnp.dot(resid.T, sketch, precision=HIGH), sketch)
    factor = jnp.linalg.cholesky(gram)
    projected = lower_solve(factor, cross.T).T
    sketch_two = time_total(jnp.dot(resid, projected, precision=HIGH))
    cross_two, gram_two = joint_total(jnp.dot(sketch_two.T, resid, precision=HIGH), sketch_two)
    factor_two = jnp.linalg.cholesky(gram_two)
    coef = lower_solve(factor_two, cross_two)
    basis_two = lower_solve(factor_two, sketch_two.T).T
    return resid - jnp.dot(basis_two, coef, precision=HIGH)


def exchange_kernel(
    peers, sides, chunk, rank,
    dil_ref, x_ref, tgt_ref, test_ref, lead_ref, trail_ref, read_ref,
    resid_ref, total_ref,
    recv, taps, pred, pred_in, tgt_in, part, part_in, red,
    own_sem, send_sem, recv_sem, tgt_send, tgt_recv, p_own, p_send, p_recv,
    s_own, s_send, s_recv, g_own, g_send, g_recv,
):
    me = lax.axis_index("tm")
    side = lax.axis_index("sens")
    other_side = 1 - side
    per = x_ref.shape[0] // peers
    steps = x_ref.shape[1]
    channels = x_ref.shape[2]
    chunks = per // chunk
    layers = lead_ref.shape[0]

    barrier = pltpu.get_barrier_semaphore()
    for k in range(1, peers):
        for s in range(sides):
            pl.semaphore_signal(barrier, inc=1, device_id={"tm": lax.rem(me + k, peers), "sens": lax.rem(side + s, sides)}, device_id_type=MESH)
    pl.semaphore_signal(barrier, inc=1, device_id={"sens": other_side}, device_id_type=MESH)
    pl.semaphore_wait(barrier, peers * sides - 1)

    def feature_copy(c, k):
        to = lax.rem(me + k, peers)
        return pltpu.make_async_remote_copy(
            src_ref=x_ref.at[pl.ds(to * per + c * chunk, chunk)],
            dst_ref=recv.at[c, me],
            send_sem=send_sem.at[c, k],
            recv_sem=recv_sem.at[c, me],
            device_id={"tm": to},
            device_id_type=MESH,
        )

    def feature_arrival(c, src):
        return pltpu.make_async_remote_copy(
            src_ref=x_ref.at[pl.ds(0, chunk)],
            dst_ref=recv.at[c, src],
            send_sem=send_sem.at[c, 1],
            recv_sem=recv_sem.at[c, src],
            device_id={"tm": lax.rem(me + 1, peers)},
            device_id_type=MESH,
        )

    def own_copy(c):
        return pltpu.make_async_copy(
            x_ref.at[pl.ds(me * per + c * chunk, chunk)], recv.at[c, me], recv_sem.at[c, me]
        )

    order = [peers // 2]
    for k in range(1, peers // 2):
        order += [peers // 2 - k, peers // 2 + k]
    for c in range(chunks):
        for k in order:
            feature_copy(c, k).start()
        own_copy(c).start()
    tgt_copy = pltpu.make_async_remote_copy(
        src_ref=tgt_ref, dst_ref=tgt_in, send_sem=tgt_send, recv_sem=tgt_recv,
        device_id={"sens": other_side}, device_id_type=MESH,
    )
    tgt_copy.start()

    for i in range(2 * layers):
        for s in range(chunk):
            taps[i, s, 0:DMAX, :] = jnp.zeros((DMAX, channels), jnp.float32)

    read = jnp.broadcast_to(read_ref[...], (16, channels))

    def conv(value, weight, i, j, dist):
        start = DMAX + j * steps
        wide = value.astype(jnp.float32)
        outs = []
        for s in range(chunk):
            taps[i, s, pl.ds(pl.multiple_of(start, DMAX), steps), :] = wide[s * steps:(s + 1) * steps]
        for s in range(chunk):
            outs.append(taps[i, s, pl.ds(start - dist, steps), :].astype(jnp.bfloat16))
        joined = jnp.concatenate([jnp.concatenate(outs, axis=0), value], axis=1)
        return jnp.dot(joined, weight, preferred_element_type=jnp.float32)

    def step(index, carry):
        c = index // peers
        j = index % peers
        feature_arrival(c, j).wait_recv()
        hidden = recv[c, j].reshape(chunk * steps, channels)
        for layer in range(layers):
            dist = dil_ref[layer]
            inner = jnp.maximum(conv(hidden, lead_ref[layer], 2 * layer, j, dist), 0.0).astype(jnp.bfloat16)
            branch = jnp.maximum(conv(inner, trail_ref[layer], 2 * layer + 1, j, dist), 0.0)
            hidden = (hidden.astype(jnp.float32) + branch).astype(jnp.bfloat16)
        for s in range(chunk):
            row = lax.dot_general(
                read, hidden[s * steps:(s + 1) * steps], (((1,), (1,)), ((), ())),
                preferred_element_type=jnp.float32,
            )
            pred[j, pl.ds(c * chunk + s, 1), :] = row[0:1, :]
        return carry

    lax.fori_loop(0, chunks * peers, step, 0)

    def pred_copy(k, s):
        to = lax.rem(me + k, peers)
        return pltpu.make_async_remote_copy(
            src_ref=pred.at[to],
            dst_ref=pred_in.at[side * peers + me],
            send_sem=p_send.at[s, k],
            recv_sem=p_recv.at[side * peers + me],
            device_id={"tm": to, "sens": lax.rem(side + s, sides)},
            device_id_type=MESH,
        )

    everyone = [(k, s) for k in range(peers) for s in range(sides) if (k, s) != (0, 0)]
    for k, s in everyone:
        pred_copy(k, s).start()
    own_pred = pltpu.make_async_copy(pred.at[me], pred_in.at[side * peers + me], p_recv.at[side * peers + me])
    own_pred.start()
    tgt_copy.wait()
    for n in range(peers * sides):
        pltpu.make_async_remote_copy(
            src_ref=pred.at[0], dst_ref=pred_in.at[n], send_sem=p_send.at[0, 1], recv_sem=p_recv.at[n],
            device_id={"sens": other_side}, device_id_type=MESH,
        ).wait_recv()
    half = peers * per
    first = side == 0
    own_target = tgt_ref[...]
    far_target = tgt_in[...]
    low = jnp.where(first, own_target, far_target)
    high = jnp.where(first, far_target, own_target)
    everything = pred_in[...].reshape(sides * half, steps)
    resid = jnp.concatenate([low, high], axis=0) - everything
    resid_ref[...] = resid
    gram = lax.dot_general(resid, resid, (((1,), (1,)), ((), ())), precision=HIGH, preferred_element_type=jnp.float32)
    sketch = lax.dot_general(resid, test_ref[...], (((1,), (1,)), ((), ())), precision=HIGH, preferred_element_type=jnp.float32)
    rows = part.shape[1]
    part[:, :, 0:sides * half] = gram.reshape(peers, rows, sides * half)
    part[:, :, sides * half:] = sketch.reshape(peers, rows, rank)

    def sum_copy(k):
        to = lax.rem(me + k, peers)
        return pltpu.make_async_remote_copy(
            src_ref=part.at[to], dst_ref=part_in.at[me], send_sem=s_send.at[k], recv_sem=s_recv.at[me],
            device_id={"tm": to}, device_id_type=MESH,
        )

    def share_copy(k):
        to = lax.rem(me + k, peers)
        return pltpu.make_async_remote_copy(
            src_ref=red, dst_ref=total_ref.at[me], send_sem=g_send.at[k], recv_sem=g_recv.at[me],
            device_id={"tm": to}, device_id_type=MESH,
        )

    for k in range(1, peers):
        sum_copy(k).start()
    own_part = pltpu.make_async_copy(part.at[me], part_in.at[me], s_recv.at[me])
    own_part.start()
    acc = None
    for n in range(peers):
        pltpu.make_async_remote_copy(
            src_ref=part.at[0], dst_ref=part_in.at[n], send_sem=s_send.at[1], recv_sem=s_recv.at[n],
            device_id={"tm": lax.rem(me + 1, peers)}, device_id_type=MESH,
        ).wait_recv()
        acc = part_in[n] if acc is None else acc + part_in[n]
    red[...] = acc
    for k in range(1, peers):
        share_copy(k).start()
    own_red = pltpu.make_async_copy(red, total_ref.at[me], g_recv.at[me])
    own_red.start()
    for n in range(peers):
        pltpu.make_async_remote_copy(
            src_ref=red, dst_ref=total_ref.at[n], send_sem=g_send.at[1], recv_sem=g_recv.at[n],
            device_id={"tm": lax.rem(me + 1, peers)}, device_id_type=MESH,
        ).wait_recv()
    for k in range(1, peers):
        for c in range(chunks):
            feature_copy(c, k).wait_send()
        sum_copy(k).wait_send()
        share_copy(k).wait_send()
    for k, s in everyone:
        pred_copy(k, s).wait_send()


def orthonormal(sketch):
    rank = sketch.shape[1]
    gram = lax.dot_general(sketch, sketch, (((0,), (0,)), ((), ())), precision=HIGH, preferred_element_type=jnp.float32)
    row_of = lax.broadcasted_iota(jnp.int32, (rank, rank), 0)
    col_of = lax.broadcasted_iota(jnp.int32, (rank, rank), 1)
    eye = jnp.where(row_of == col_of, 1.0, 0.0).astype(jnp.float32)
    both = jnp.concatenate([gram, eye], axis=1)
    blocks = [both[8 * b:8 * b + 8] for b in range(rank // 8)]
    sub = lax.broadcasted_iota(jnp.int32, (8, 2 * rank), 0)

    def spread(block, k):
        return jnp.broadcast_to(block[:, k:k + 1], block.shape)

    for k in range(0, rank, 2):
        top, at = k // 8, k % 8
        row, after = blocks[top][at:at + 1, :], blocks[top][at + 1:at + 2, :]
        inverse = 1.0 / spread(row, k)
        cross = spread(row, k + 1)
        lower = spread(after, k) * inverse
        upper = cross * inverse
        inverse_after = 1.0 / (spread(after, k + 1) - lower * cross)
        scaled = row * inverse
        scaled_after = (after - lower * row) * inverse_after
        for b in range(top, rank // 8):
            col = spread(blocks[b], k)
            col_after = spread(blocks[b], k + 1) - col * upper
            if b == top:
                col = jnp.where(sub > at, col, 0.0)
                col_after = jnp.where(sub > at + 1, col_after, 0.0)
            blocks[b] = blocks[b] - col * scaled - col_after * scaled_after
    both = jnp.concatenate(blocks, axis=0)
    pivots = jnp.sum(jnp.where(row_of == col_of, both[:, :rank], 0.0), axis=1, keepdims=True)
    inverse_factor = both[:, rank:] * (1.0 / jnp.sqrt(pivots))
    return lax.dot_general(sketch, inverse_factor, (((1,), (1,)), ((), ())), precision=HIGH, preferred_element_type=jnp.float32)


def finish_kernel(own, resid_ref, total_ref, out_ref, basis_ref):
    side = lax.axis_index("sens")
    total = total_ref[...].reshape(resid_ref.shape[0], total_ref.shape[2])
    size = resid_ref.shape[0]
    gram = total[:, :size]
    basis = orthonormal(total[:, size:])
    sketch = jnp.dot(gram, basis, precision=HIGH, preferred_element_type=jnp.float32)
    basis = orthonormal(sketch)
    basis_ref[...] = basis
    resid = resid_ref[...]
    coef = lax.dot_general(basis, resid, (((0,), (0,)), ((), ())), precision=HIGH, preferred_element_type=jnp.float32)
    mine = pl.ds(pl.multiple_of(side * own, own), own)
    out_ref[...] = resid_ref[mine, :] - jnp.dot(basis_ref[mine, :], coef, precision=HIGH, preferred_element_type=jnp.float32)


def sensor_form(
    features, target, test_matrix, leading_conv_taps, trailing_conv_taps, readout, dilations
):
    peers = lax.axis_size("tm")
    sides = lax.axis_size("sens")
    own, steps, channels = features.shape
    rank = test_matrix.shape[1]
    layers = leading_conv_taps.shape[0]
    per = own // peers
    chunk = 2 if per % 2 == 0 else 1
    chunks = per // chunk
    size = own * sides
    lead = leading_conv_taps.reshape(layers, 2 * channels, channels)
    trail = trailing_conv_taps.reshape(layers, 2 * channels, channels)
    read = readout.reshape(1, channels)
    vmem = pl.BlockSpec(memory_space=pltpu.VMEM)
    dma = pltpu.SemaphoreType.DMA
    resid, total = pl.pallas_call(
        functools.partial(exchange_kernel, peers, sides, chunk, rank),
        out_shape=(
            jax.ShapeDtypeStruct((size, steps), jnp.float32),
            jax.ShapeDtypeStruct((peers, size // peers, size + rank), jnp.float32),
        ),
        in_specs=[
            pl.BlockSpec(memory_space=pltpu.SMEM), pl.BlockSpec(memory_space=pl.ANY),
            vmem, vmem, vmem, vmem, vmem,
        ],
        out_specs=(vmem, vmem),
        scratch_shapes=[
            pltpu.VMEM((chunks, peers, chunk, steps, channels), jnp.bfloat16),
            pltpu.VMEM((2 * layers, chunk, DMAX + peers * steps, channels), jnp.float32),
            pltpu.VMEM((peers, per, steps), jnp.float32),
            pltpu.VMEM((peers * sides, per, steps), jnp.float32),
            pltpu.VMEM((own, steps), jnp.float32),
            pltpu.VMEM((peers, size // peers, size + rank), jnp.float32),
            pltpu.VMEM((peers, size // peers, size + rank), jnp.float32),
            pltpu.VMEM((size // peers, size + rank), jnp.float32),
            dma, dma((chunks, peers)), dma((chunks, peers)), dma, dma,
            dma, dma((sides, peers)), dma((peers * sides,)),
            dma, dma((peers,)), dma((peers,)),
            dma, dma((peers,)), dma((peers,)),
        ],
        compiler_params=pltpu.CompilerParams(
            collective_id=0, has_side_effects=True, vmem_limit_bytes=56 * 1024 * 1024
        ),
        name="exchange",
    )(dilations, features, target, test_matrix.T, lead, trail, read)
    return pl.pallas_call(
        functools.partial(finish_kernel, own),
        out_shape=jax.ShapeDtypeStruct((own, steps), jnp.float32),
        in_specs=[vmem, vmem],
        out_specs=vmem,
        scratch_shapes=[pltpu.VMEM((size, rank), jnp.float32)],
        name="finish",
    )(resid, total)


def on_device(features, *rest):
    peers = lax.axis_size("tm")
    if lax.axis_size("sens") == 2 and features.shape[0] % (8 * peers) == 0:
        return sensor_form(features, *rest)
    return halo_form(features, *rest)


def solution(mesh):
    placed = (
        P(("grp", "sens"), "tm", None),
        P(("grp", "sens"), "tm"),
        P("tm", None),
        P(),
        P(),
        P(),
        P(),
    )
    return jax.shard_map(
        on_device, mesh=mesh, in_specs=placed, out_specs=P(("grp", "sens"), "tm"), check_vma=False
    )
```

```python
import functools

import jax
import jax.numpy as jnp
from jax import lax
from jax.experimental import pallas as pl
from jax.experimental.pallas import tpu as pltpu
from jax.sharding import PartitionSpec as P

DMAX = 128
MESH = pl.DeviceIdType.MESH
HIGH = lax.Precision.HIGHEST


def shifted(value, axis, by):
    peers = lax.axis_size(axis)
    pairs = [(i, i + by) for i in range(peers) if 0 <= i + by < peers]
    return lax.ppermute(value, axis, pairs)


def dilated(before, current, dist, weight):
    extended = jnp.concatenate([before, current], axis=1)
    moved = lax.dynamic_slice_in_dim(extended, before.shape[1] - dist, current.shape[1], 1)
    total = jnp.einsum("stc,cd->std", moved, weight[0], preferred_element_type=jnp.float32)
    return total + jnp.einsum("stc,cd->std", current, weight[1], preferred_element_type=jnp.float32)


def causal_tail(value):
    return shifted(value[:, -DMAX:, :], "tm", 1)


def time_total(value):
    return lax.psum(value, "tm")


def joint_total(cross, sketch):
    return lax.psum((cross, jnp.dot(sketch.T, sketch, precision=HIGH)), "sens")


def lower_solve(factor, value):
    return jax.scipy.linalg.solve_triangular(factor, value, lower=True)


def halo_form(
    features, target, test_matrix, leading_conv_taps, trailing_conv_taps, readout, dilations
):
    hidden = features
    for layer in range(leading_conv_taps.shape[0]):
        dist = dilations[layer]
        inner = jax.nn.relu(
            dilated(causal_tail(hidden), hidden, dist, leading_conv_taps[layer])
        ).astype(jnp.bfloat16)
        branch = jax.nn.relu(dilated(causal_tail(inner), inner, dist, trailing_conv_taps[layer]))
        hidden = (hidden.astype(jnp.float32) + branch).astype(jnp.bfloat16)
    prediction_values = jnp.einsum("stc,c->st", hidden, readout, preferred_element_type=jnp.float32)
    resid = target - prediction_values
    sketch = time_total(jnp.dot(resid, test_matrix, precision=HIGH))
    cross, gram = joint_total(jnp.dot(resid.T, sketch, precision=HIGH), sketch)
    factor = jnp.linalg.cholesky(gram)
    projected = lower_solve(factor, cross.T).T
    sketch_two = time_total(jnp.dot(resid, projected, precision=HIGH))
    cross_two, gram_two = joint_total(jnp.dot(sketch_two.T, resid, precision=HIGH), sketch_two)
    factor_two = jnp.linalg.cholesky(gram_two)
    coef = lower_solve(factor_two, cross_two)
    basis_two = lower_solve(factor_two, sketch_two.T).T
    return resid - jnp.dot(basis_two, coef, precision=HIGH)


def exchange_kernel(
    peers, sides, chunk, rank,
    dil_ref, x_ref, tgt_ref, test_ref, lead_ref, trail_ref, read_ref,
    resid_ref, total_ref,
    recv, taps, last, pred, pred_in, tgt_in, part, part_in, red,
    own_sem, send_sem, recv_sem, tgt_send, tgt_recv, p_own, p_send, p_recv,
    s_own, s_send, s_recv, g_own, g_send, g_recv,
):
    me = lax.axis_index("tm")
    side = lax.axis_index("sens")
    other_side = 1 - side
    per = x_ref.shape[0] // peers
    steps = x_ref.shape[1]
    channels = x_ref.shape[2]
    chunks = per // chunk
    layers = lead_ref.shape[0]

    barrier = pltpu.get_barrier_semaphore()
    for k in range(1, peers):
        for s in range(sides):
            pl.semaphore_signal(barrier, inc=1, device_id={"tm": lax.rem(me + k, peers), "sens": lax.rem(side + s, sides)}, device_id_type=MESH)
    pl.semaphore_signal(barrier, inc=1, device_id={"sens": other_side}, device_id_type=MESH)
    pl.semaphore_wait(barrier, peers * sides - 1)

    def feature_copy(c, k):
        to = lax.rem(me + k, peers)
        return pltpu.make_async_remote_copy(
            src_ref=x_ref.at[pl.ds(to * per + c * chunk, chunk)],
            dst_ref=recv.at[c, me],
            send_sem=send_sem.at[c, k],
            recv_sem=recv_sem.at[c, me],
            device_id={"tm": to},
            device_id_type=MESH,
        )

    def feature_arrival(c, src):
        return pltpu.make_async_remote_copy(
            src_ref=x_ref.at[pl.ds(0, chunk)],
            dst_ref=recv.at[c, src],
            send_sem=send_sem.at[c, 1],
            recv_sem=recv_sem.at[c, src],
            device_id={"tm": lax.rem(me + 1, peers)},
            device_id_type=MESH,
        )

    def own_copy(c):
        return pltpu.make_async_copy(
            x_ref.at[pl.ds(me * per + c * chunk, chunk)], recv.at[c, me], recv_sem.at[c, me]
        )

    order = [peers // 2]
    for k in range(1, peers // 2):
        order += [peers // 2 - k, peers // 2 + k]
    for c in range(chunks):
        for k in order:
            feature_copy(c, k).start()
        own_copy(c).start()
    tgt_copy = pltpu.make_async_remote_copy(
        src_ref=tgt_ref, dst_ref=tgt_in, send_sem=tgt_send, recv_sem=tgt_recv,
        device_id={"sens": other_side}, device_id_type=MESH,
    )
    tgt_copy.start()

    for i in range(2 * layers):
        for s in range(chunk):
            taps[i, s, 0:DMAX, :] = jnp.zeros((DMAX, channels), jnp.float32)

    read = jnp.broadcast_to(read_ref[...], (16, channels))

    def conv(value, weight, i, j, dist):
        start = DMAX + j * steps
        wide = value.astype(jnp.float32)
        outs = []
        for s in range(chunk):
            taps[i, s, pl.ds(pl.multiple_of(start, DMAX), steps), :] = wide[s * steps:(s + 1) * steps]
        for s in range(chunk):
            outs.append(taps[i, s, pl.ds(start - dist, steps), :].astype(jnp.bfloat16))
        joined = jnp.concatenate([jnp.concatenate(outs, axis=0), value], axis=1)
        return jnp.dot(joined, weight, preferred_element_type=jnp.float32)

    last[...] = jnp.zeros_like(last)

    def readout_of(index):
        c = index // peers
        j = index % peers
        row = lax.dot_general(
            read, last[...], (((1,), (1,)), ((), ())), preferred_element_type=jnp.float32
        )
        for s in range(chunk):
            pred[j, pl.ds(c * chunk + s, 1), :] = row[0:1, s * steps:(s + 1) * steps]

    def step(index, carry):
        c = index // peers
        j = index % peers
        feature_arrival(c, j).wait_recv()
        readout_of((index + chunks * peers - 1) % (chunks * peers))
        hidden = recv[c, j].reshape(chunk * steps, channels)
        for layer in range(layers):
            dist = dil_ref[layer]
            inner = jnp.maximum(conv(hidden, lead_ref[layer], 2 * layer, j, dist), 0.0).astype(jnp.bfloat16)
            branch = jnp.maximum(conv(inner, trail_ref[layer], 2 * layer + 1, j, dist), 0.0)
            hidden = (hidden.astype(jnp.float32) + branch).astype(jnp.bfloat16)
        last[...] = hidden
        return carry

    lax.fori_loop(0, chunks * peers, step, 0)
    readout_of(chunks * peers - 1)

    def pred_copy(k, s):
        to = lax.rem(me + k, peers)
        return pltpu.make_async_remote_copy(
            src_ref=pred.at[to],
            dst_ref=pred_in.at[side * peers + me],
            send_sem=p_send.at[s, k],
            recv_sem=p_recv.at[side * peers + me],
            device_id={"tm": to, "sens": lax.rem(side + s, sides)},
            device_id_type=MESH,
        )

    everyone = [(k, s) for k in range(peers) for s in range(sides) if (k, s) != (0, 0)]
    for k, s in everyone:
        pred_copy(k, s).start()
    own_pred = pltpu.make_async_copy(pred.at[me], pred_in.at[side * peers + me], p_recv.at[side * peers + me])
    own_pred.start()
    tgt_copy.wait()
    for n in range(peers * sides):
        pltpu.make_async_remote_copy(
            src_ref=pred.at[0], dst_ref=pred_in.at[n], send_sem=p_send.at[0, 1], recv_sem=p_recv.at[n],
            device_id={"sens": other_side}, device_id_type=MESH,
        ).wait_recv()
    half = peers * per
    first = side == 0
    own_target = tgt_ref[...]
    far_target = tgt_in[...]
    low = jnp.where(first, own_target, far_target)
    high = jnp.where(first, far_target, own_target)
    everything = pred_in[...].reshape(sides * half, steps)
    resid = jnp.concatenate([low, high], axis=0) - everything
    resid_ref[...] = resid
    gram = lax.dot_general(resid, resid, (((1,), (1,)), ((), ())), precision=HIGH, preferred_element_type=jnp.float32)
    sketch = lax.dot_general(resid, test_ref[...], (((1,), (1,)), ((), ())), precision=HIGH, preferred_element_type=jnp.float32)
    rows = part.shape[1]
    part[:, :, 0:sides * half] = gram.reshape(peers, rows, sides * half)
    part[:, :, sides * half:] = sketch.reshape(peers, rows, rank)

    def sum_copy(k):
        to = lax.rem(me + k, peers)
        return pltpu.make_async_remote_copy(
            src_ref=part.at[to], dst_ref=part_in.at[me], send_sem=s_send.at[k], recv_sem=s_recv.at[me],
            device_id={"tm": to}, device_id_type=MESH,
        )

    def share_copy(k):
        to = lax.rem(me + k, peers)
        return pltpu.make_async_remote_copy(
            src_ref=red, dst_ref=total_ref.at[me], send_sem=g_send.at[k], recv_sem=g_recv.at[me],
            device_id={"tm": to}, device_id_type=MESH,
        )

    for k in range(1, peers):
        sum_copy(k).start()
    own_part = pltpu.make_async_copy(part.at[me], part_in.at[me], s_recv.at[me])
    own_part.start()
    acc = None
    for n in range(peers):
        pltpu.make_async_remote_copy(
            src_ref=part.at[0], dst_ref=part_in.at[n], send_sem=s_send.at[1], recv_sem=s_recv.at[n],
            device_id={"tm": lax.rem(me + 1, peers)}, device_id_type=MESH,
        ).wait_recv()
        acc = part_in[n] if acc is None else acc + part_in[n]
    red[...] = acc
    for k in range(1, peers):
        share_copy(k).start()
    own_red = pltpu.make_async_copy(red, total_ref.at[me], g_recv.at[me])
    own_red.start()
    for n in range(peers):
        pltpu.make_async_remote_copy(
            src_ref=red, dst_ref=total_ref.at[n], send_sem=g_send.at[1], recv_sem=g_recv.at[n],
            device_id={"tm": lax.rem(me + 1, peers)}, device_id_type=MESH,
        ).wait_recv()
    for k in range(1, peers):
        for c in range(chunks):
            feature_copy(c, k).wait_send()
        sum_copy(k).wait_send()
        share_copy(k).wait_send()
    for k, s in everyone:
        pred_copy(k, s).wait_send()


def orthonormal(sketch):
    rank = sketch.shape[1]
    gram = lax.dot_general(sketch, sketch, (((0,), (0,)), ((), ())), precision=HIGH, preferred_element_type=jnp.float32)
    row_of = lax.broadcasted_iota(jnp.int32, (rank, rank), 0)
    col_of = lax.broadcasted_iota(jnp.int32, (rank, rank), 1)
    eye = jnp.where(row_of == col_of, 1.0, 0.0).astype(jnp.float32)
    both = jnp.concatenate([gram, eye], axis=1)
    blocks = [both[8 * b:8 * b + 8] for b in range(rank // 8)]
    sub = lax.broadcasted_iota(jnp.int32, (8, 2 * rank), 0)

    def spread(block, k):
        return jnp.broadcast_to(block[:, k:k + 1], block.shape)

    for k in range(0, rank, 2):
        top, at = k // 8, k % 8
        row, after = blocks[top][at:at + 1, :], blocks[top][at + 1:at + 2, :]
        inverse = 1.0 / spread(row, k)
        cross = spread(row, k + 1)
        lower = spread(after, k) * inverse
        upper = cross * inverse
        inverse_after = 1.0 / (spread(after, k + 1) - lower * cross)
        scaled = row * inverse
        scaled_after = (after - lower * row) * inverse_after
        for b in range(top, rank // 8):
            col = spread(blocks[b], k)
            col_after = spread(blocks[b], k + 1) - col * upper
            if b == top:
                col = jnp.where(sub > at, col, 0.0)
                col_after = jnp.where(sub > at + 1, col_after, 0.0)
            blocks[b] = blocks[b] - col * scaled - col_after * scaled_after
    both = jnp.concatenate(blocks, axis=0)
    pivots = jnp.sum(jnp.where(row_of == col_of, both[:, :rank], 0.0), axis=1, keepdims=True)
    inverse_factor = both[:, rank:] * (1.0 / jnp.sqrt(pivots))
    return lax.dot_general(sketch, inverse_factor, (((1,), (1,)), ((), ())), precision=HIGH, preferred_element_type=jnp.float32)


def finish_kernel(own, resid_ref, total_ref, out_ref, basis_ref):
    side = lax.axis_index("sens")
    total = total_ref[...].reshape(resid_ref.shape[0], total_ref.shape[2])
    size = resid_ref.shape[0]
    gram = total[:, :size]
    basis = orthonormal(total[:, size:])
    sketch = jnp.dot(gram, basis, precision=HIGH, preferred_element_type=jnp.float32)
    basis = orthonormal(sketch)
    basis_ref[...] = basis
    resid = resid_ref[...]
    coef = lax.dot_general(basis, resid, (((0,), (0,)), ((), ())), precision=HIGH, preferred_element_type=jnp.float32)
    mine = pl.ds(pl.multiple_of(side * own, own), own)
    out_ref[...] = resid_ref[mine, :] - jnp.dot(basis_ref[mine, :], coef, precision=HIGH, preferred_element_type=jnp.float32)


def sensor_form(
    features, target, test_matrix, leading_conv_taps, trailing_conv_taps, readout, dilations
):
    peers = lax.axis_size("tm")
    sides = lax.axis_size("sens")
    own, steps, channels = features.shape
    rank = test_matrix.shape[1]
    layers = leading_conv_taps.shape[0]
    per = own // peers
    chunk = 2 if per % 2 == 0 else 1
    chunks = per // chunk
    size = own * sides
    lead = leading_conv_taps.reshape(layers, 2 * channels, channels)
    trail = trailing_conv_taps.reshape(layers, 2 * channels, channels)
    read = readout.reshape(1, channels)
    vmem = pl.BlockSpec(memory_space=pltpu.VMEM)
    dma = pltpu.SemaphoreType.DMA
    resid, total = pl.pallas_call(
        functools.partial(exchange_kernel, peers, sides, chunk, rank),
        out_shape=(
            jax.ShapeDtypeStruct((size, steps), jnp.float32),
            jax.ShapeDtypeStruct((peers, size // peers, size + rank), jnp.float32),
        ),
        in_specs=[
            pl.BlockSpec(memory_space=pltpu.SMEM), pl.BlockSpec(memory_space=pl.ANY),
            vmem, vmem, vmem, vmem, vmem,
        ],
        out_specs=(vmem, vmem),
        scratch_shapes=[
            pltpu.VMEM((chunks, peers, chunk, steps, channels), jnp.bfloat16),
            pltpu.VMEM((2 * layers, chunk, DMAX + peers * steps, channels), jnp.float32),
            pltpu.VMEM((chunk * steps, channels), jnp.bfloat16),
            pltpu.VMEM((peers, per, steps), jnp.float32),
            pltpu.VMEM((peers * sides, per, steps), jnp.float32),
            pltpu.VMEM((own, steps), jnp.float32),
            pltpu.VMEM((peers, size // peers, size + rank), jnp.float32),
            pltpu.VMEM((peers, size // peers, size + rank), jnp.float32),
            pltpu.VMEM((size // peers, size + rank), jnp.float32),
            dma, dma((chunks, peers)), dma((chunks, peers)), dma, dma,
            dma, dma((sides, peers)), dma((peers * sides,)),
            dma, dma((peers,)), dma((peers,)),
            dma, dma((peers,)), dma((peers,)),
        ],
        compiler_params=pltpu.CompilerParams(
            collective_id=0, has_side_effects=True, vmem_limit_bytes=56 * 1024 * 1024
        ),
        name="exchange",
    )(dilations, features, target, test_matrix.T, lead, trail, read)
    return pl.pallas_call(
        functools.partial(finish_kernel, own),
        out_shape=jax.ShapeDtypeStruct((own, steps), jnp.float32),
        in_specs=[vmem, vmem],
        out_specs=vmem,
        scratch_shapes=[pltpu.VMEM((size, rank), jnp.float32)],
        name="finish",
    )(resid, total)


def on_device(features, *rest):
    peers = lax.axis_size("tm")
    if lax.axis_size("sens") == 2 and features.shape[0] % (8 * peers) == 0:
        return sensor_form(features, *rest)
    return halo_form(features, *rest)


def solution(mesh):
    placed = (
        P(("grp", "sens"), "tm", None),
        P(("grp", "sens"), "tm"),
        P("tm", None),
        P(),
        P(),
        P(),
        P(),
    )
    return jax.shard_map(
        on_device, mesh=mesh, in_specs=placed, out_specs=P(("grp", "sens"), "tm"), check_vma=False
    )
```
